256 devices in a mesh: leaf: 64 (over y_lo, x, z), rhs: 4 (over y_hi, core).
Axes of the slice: x: 4, y: 4 (y_hi: 2, y_lo: 2; y = y_hi * 2 + y_lo), z: 8, core: 2. Of those that a mesh axis runs over, the one named last changes fastest.
Arguments:
- right_sides: bfloat16 [65536, 4096], P('leaf', 'rhs'), may hold values from -6 to 6
- leaf_inverse: bfloat16 [65536, 1024], P(('leaf', 'rhs')), may hold values from -0.1875 to 0.1875
- project_factors: bfloat16 [3, 65536, 128], P(None, 'leaf'), may hold values from -0.1875 to 0.1875
- correct_factors: bfloat16 [3, 65536, 128], P(None, 'leaf'), may hold values from -0.5 to 0.5
- coupling_first: bfloat16 [32, 256, 256], P(None, 'rhs'), may hold values from -0.375 to 0.375
- coupling_second: bfloat16 [16, 256, 256], P(None, 'rhs'), may hold values from -0.375 to 0.375
- coupling_third: bfloat16 [8, 256, 256], P(None, 'rhs'), may hold values from -0.375 to 0.375
Outputs:
- solution: bfloat16 [65536, 4096], P('leaf', 'rhs')
The draws below stay inside these ranges and needn't reach their ends.
All inputs are finite; a program needn't handle non-finite values.
Results may differ from the reference program's by a relative error of at most 0.014.
Values may be sent and summed in bfloat16 or wider, within the bound.
No kernel may reach another device: no remote copies, remote signals or barrier semaphores. Data moves between devices by JAX's collectives and lax.ppermute only.
A program may use at most 64 MiB of HBM per device.

```python
import jax
import jax.numpy as jnp
from jax import lax

LEAF = 1024
R = 128
LEVELS = 3
ORDER = 65536
COLS = 4096
N_LEAF = 64


def block_levels(key, dims, split, low, high):
    loudness, own = 1.0, jax.random.fold_in(key, 6)
    for axis_at, blocks in split:
        draws = jnp.exp(jax.random.uniform(jax.random.fold_in(own, axis_at), (blocks,), jnp.float32, low / len(split), high / len(split)))
        loudness = loudness * jnp.repeat(draws, dims[axis_at] // blocks).reshape([-1 if axis == axis_at else 1 for axis in range(len(dims))])
    return loudness


def normal_values(key, shape, spread, reach, shards=(), dtype=jnp.bfloat16):
    result = jax.random.normal(key, shape, jnp.float32) * spread
    if len(shards) > 0:
        result = block_levels(key, shape, shards, -0.22, 0.18) * result
    return jnp.clip(result, min=-reach, max=reach).astype(dtype)


def setup_inputs(seed: int = 0) -> dict:
    key_of = jax.random.split(jax.random.key(seed), 8)
    right_sides = normal_values(key_of[0], (ORDER, COLS), 1.0, 6.0, ((0, 64), (1, 4)))
    leaf_inverse = normal_values(key_of[1], (ORDER, LEAF), LEAF ** -0.5, 0.1875, ((0, 256),))
    project_factors = normal_values(key_of[2], (LEVELS, ORDER, R), LEAF ** -0.5, 0.1875, ((1, 64),))
    correct_factors = normal_values(key_of[3], (LEVELS, ORDER, R), R ** -0.5, 0.5, ((1, 64),))
    coupling_first = normal_values(key_of[4], (N_LEAF // 2, 2 * R, 2 * R), (2 * R) ** -0.5, 0.375, ((1, 4),))
    coupling_second = normal_values(key_of[5], (N_LEAF // 4, 2 * R, 2 * R), (2 * R) ** -0.5, 0.375, ((1, 4),))
    coupling_third = normal_values(key_of[6], (N_LEAF // 8, 2 * R, 2 * R), (2 * R) ** -0.5, 0.375, ((1, 4),))
    return dict(right_sides=right_sides, leaf_inverse=leaf_inverse, project_factors=project_factors, correct_factors=correct_factors, coupling_first=coupling_first, coupling_second=coupling_second, coupling_third=coupling_third)


def leaf_products(left, right):
    return lax.map(lambda pair: jnp.dot(pair[0], pair[1], preferred_element_type=jnp.float32), (left, right))


def reference(right_sides, leaf_inverse, project_factors, correct_factors, coupling_first, coupling_second, coupling_third):
    count = ORDER // LEAF
    blocks = right_sides.reshape(count, LEAF, COLS)
    inverse = leaf_inverse.reshape(count, LEAF, LEAF)
    start = leaf_products(inverse, blocks).astype(jnp.bfloat16)
    current = start.astype(jnp.float32)
    tables = (coupling_first, coupling_second, coupling_third)
    for level in range(LEVELS):
        rounded = current.astype(jnp.bfloat16)
        factors = project_factors[level].reshape(count, LEAF, R)
        terms = lax.map(lambda pair: jnp.dot(pair[0].T, pair[1], preferred_element_type=jnp.float32), (factors, rounded))
        group = 2 ** level
        projection = jnp.sum(terms.reshape(count // group, group, R, COLS), axis=1).astype(jnp.bfloat16)
        nodes = count // (2 * group)
        stacked = projection.reshape(nodes, 2 * R, COLS)
        answer = leaf_products(tables[level], stacked).astype(jnp.bfloat16)
        children = answer.reshape(2 * nodes, R, COLS)
        per_leaf = jnp.repeat(children, group, axis=0)
        left = correct_factors[level].reshape(count, LEAF, R)
        current = current - leaf_products(left, per_leaf)
    return current.reshape(ORDER, COLS).astype(jnp.bfloat16)
```

```python
import functools

import jax
import jax.numpy as jnp
from jax import lax
from jax.experimental import pallas as pl
from jax.experimental.pallas import tpu as pltpu
from jax.sharding import PartitionSpec as P

BF = jnp.bfloat16
F32 = jnp.float32
VMEM = pl.BlockSpec(memory_space=pltpu.VMEM)
SMEM = pl.BlockSpec(memory_space=pltpu.SMEM)


def partner(value, axis, mask):
    pairs = [(source, source ^ mask) for source in range(lax.axis_size(axis))]
    return lax.ppermute(value, axis, pairs)


def mm(a, b):
    return lax.dot_general(a, b, (((1,), (0,)), ((), ())), preferred_element_type=F32)


def mm_nt(a, b):
    return lax.dot_general(a, b, (((1,), (1,)), ((), ())), preferred_element_type=F32)


def mm_tn(a, b):
    return lax.dot_general(a, b, (((0,), (0,)), ((), ())), preferred_element_type=F32)


def call(body, outs, args, flops, scratch=(), limit=8 << 20, name=None):
    outs = [jax.ShapeDtypeStruct(s, d) for s, d in outs]
    size = sum(a.size * a.dtype.itemsize for a in args) + sum(
        o.size * o.dtype.itemsize for o in outs
    )
    specs = [SMEM if a.dtype == jnp.int32 else VMEM for a in args]
    return pl.pallas_call(
        body,
        out_shape=outs,
        in_specs=specs,
        out_specs=[VMEM] * len(outs),
        scratch_shapes=list(scratch),
        cost_estimate=pl.CostEstimate(flops=flops, bytes_accessed=size, transcendentals=0),
        compiler_params=pltpu.CompilerParams(vmem_limit_bytes=limit),
        name=name,
    )(*args)


def cross_kernel(p_ref, c_ref, m_ref):
    m_ref[0] = mm_tn(p_ref[1], c_ref[0]).astype(BF)
    m_ref[1] = mm_tn(p_ref[2], c_ref[0]).astype(BF)
    m_ref[2] = mm_tn(p_ref[2], c_ref[1]).astype(BF)


def couple_kernel(idx_ref, k0_ref, k1_ref, k2_ref, k3_ref, m_ref, mt_ref, k_ref, gh_ref, n_ref):
    r, b0 = idx_ref[0], idx_ref[1]
    for k, ref in enumerate((k0_ref, k1_ref, k2_ref, k3_ref)):
        at = pl.multiple_of((r ^ k) * 64, 64)
        for level in range(3):
            k_ref[level, pl.ds(at, 64), :] = ref[level]
    cols = pl.ds(pl.multiple_of(b0 * 128, 128), 128)
    mine = k_ref[0, pl.ds(pl.multiple_of(b0 * 128, 128), 128), cols]
    other = k_ref[0, pl.ds(pl.multiple_of((1 - b0) * 128, 128), 128), cols]
    for i in range(2):
        gh_ref[i] = (mm(m_ref[i], mine) + mm(mt_ref[i], other)).astype(BF)
    n_ref[...] = (m_ref[2].astype(F32) + mt_ref[2].astype(F32)).astype(BF)


def factor_kernel(idx_ref, k_ref, gh_ref, n_ref, nt_ref, p_ref, out_ref):
    b1 = idx_ref[2]
    cols = pl.ds(pl.multiple_of(b1 * 128, 128), 128)
    mine = k_ref[1, pl.ds(pl.multiple_of(b1 * 128, 128), 128), cols]
    other = k_ref[1, pl.ds(pl.multiple_of((1 - b1) * 128, 128), 128), cols]
    low = mm(n_ref[...], mine) + mm(nt_ref[...], other)
    low_b = low.astype(BF)
    g, h = gh_ref[0], gh_ref[1]
    skip = (mm(low_b, g) - h.astype(F32)).astype(BF)
    rows = lax.broadcasted_iota(jnp.int32, (128, 128), 0)
    eye = (rows == lax.broadcasted_iota(jnp.int32, (128, 128), 1)).astype(BF)
    out_ref[0:128] = mm_nt(eye, p_ref[0]).astype(BF)
    out_ref[128:256] = (mm_nt(eye, p_ref[1]) - mm_nt(g, p_ref[0])).astype(BF)
    out_ref[256:384] = (
        mm_nt(eye, p_ref[2]) - mm_nt(low_b, p_ref[1]) + mm_nt(skip, p_ref[0])
    ).astype(BF)


def project_kernel(idx_ref, f_ref, s0, s1, s2, s3, p0_ref, send2, send1, keep2, keep1):
    r, b0 = idx_ref[0], idx_ref[1]
    for part in range(2):
        half = b0 ^ (1 - part)
        cols = pl.ds(pl.multiple_of(half * 512, 512), 512)
        total = None
        for k, ref in enumerate((s0, s1, s2, s3)):
            rows = pl.ds(pl.multiple_of((r ^ k) * 256, 256), 256)
            term = mm(f_ref[:, rows], ref[:, cols])
            total = term if total is None else total + term
        p0_ref[:, cols] = total[0:128].astype(BF)
        if part == 0:
            send1[...] = total[128:256].astype(BF)
            send2[...] = total[256:384].astype(BF)
        else:
            keep1[...] = total[128:256]
            keep2[...] = total[256:384]


def sum2a_kernel(idx_ref, keep_ref, recv_ref, send_ref, mine_ref):
    b1 = idx_ref[2]
    own = pl.ds(pl.multiple_of(b1 * 256, 256), 256)
    other = pl.ds(pl.multiple_of((1 - b1) * 256, 256), 256)
    send_ref[...] = (keep_ref[:, other] + recv_ref[:, other].astype(F32)).astype(BF)
    mine_ref[...] = keep_ref[:, own] + recv_ref[:, own].astype(F32)


def sum1_kernel(keep_ref, recv_ref, out_ref):
    out_ref[...] = (keep_ref[...] + recv_ref[...].astype(F32)).astype(BF)


def answer_kernel(level, idx_ref, k_ref, mine_ref, other_ref, out_ref):
    bit = idx_ref[1 + level]
    rows = pl.ds(pl.multiple_of(bit * 128, 128), 128)
    own = k_ref[level, rows, pl.ds(pl.multiple_of(bit * 128, 128), 128)]
    other = k_ref[level, rows, pl.ds(pl.multiple_of((1 - bit) * 128, 128), 128)]
    out_ref[...] = (mm(own, mine_ref[...]) + mm(other, other_ref[...])).astype(BF)


def join_kernel(idx_ref, own_ref, recv_ref, out_ref):
    b1 = idx_ref[2]
    out_ref[:, pl.ds(pl.multiple_of(b1 * 256, 256), 256)] = own_ref[...]
    out_ref[:, pl.ds(pl.multiple_of((1 - b1) * 256, 256), 256)] = recv_ref[...]


def final_kernel(idx_ref, s0, s1, s2, s3, c_ref, a0, a1h, a1o, a2h, a2o, out_ref):
    r, b0 = idx_ref[0], idx_ref[1]
    for part, (a1, a2) in enumerate(((a1h, a2h), (a1o, a2o))):
        cols = pl.ds(pl.multiple_of((b0 ^ part) * 512, 512), 512)
        for k, ref in enumerate((s0, s1, s2, s3)):
            rows = pl.ds(pl.multiple_of((r ^ k) * 256, 256), 256)
            value = ref[:, cols].astype(F32) - mm(c_ref[0, rows], a0[:, cols])
            value = value - mm(c_ref[1, rows], a1[...])
            value = value - mm(c_ref[2, rows], a2[...])
            out_ref[rows, cols] = value.astype(BF)


def local(right, inverse, project, correct, first, second, third):
    leaf, r = lax.axis_index("leaf"), lax.axis_index("rhs")
    idx = jnp.stack([r, leaf & 1, leaf >> 1 & 1, leaf >> 2 & 1]).astype(jnp.int32)

    inv_y = partner(inverse, "rhs", 2)
    inv_c = partner(inverse, "rhs", 1)
    nodes = jnp.stack(
        [
            lax.dynamic_slice_in_dim(table, leaf >> level + 1, 1, 0)[0]
            for level, table in enumerate((first, second, third))
        ]
    )
    nodes_y = partner(nodes, "rhs", 2)
    nodes_c = partner(nodes, "rhs", 1)
    nodes_yc = partner(nodes_y, "rhs", 1)
    inv_yc = partner(inv_y, "rhs", 1)

    (cross,) = call(
        cross_kernel, [((3, 128, 128), BF)], (project, correct), 3 * 2 * 128 * 128 * 1024, name="cross"
    )
    cross_t = partner(cross, "leaf", 1)
    table, gh, low = call(
        couple_kernel,
        [((3, 256, 256), BF), ((2, 128, 128), BF), ((128, 128), BF)],
        (idx, nodes, nodes_c, nodes_y, nodes_yc, cross, cross_t),
        8 * 128**3,
        name="couple",
    )
    low_t = partner(low, "leaf", 2)
    (factors,) = call(
        factor_kernel,
        [((384, 1024), BF)],
        (idx, table, gh, low, low_t, project),
        12 * 128 * 128 * 1024,
        name="factor",
    )

    starts = [
        jnp.dot(block, right, preferred_element_type=F32).astype(BF)
        for block in (inverse, inv_c, inv_y, inv_yc)
    ]
    p0, send2, send1, keep2, keep1 = call(
        project_kernel,
        [
            ((128, 1024), BF),
            ((128, 512), BF),
            ((128, 512), BF),
            ((128, 512), F32),
            ((128, 512), F32),
        ],
        (idx, factors, *starts),
        2 * 384 * 1024 * 1024,
        name="project",
    )
    recv2 = partner(send2, "leaf", 1)
    recv1 = partner(send1, "leaf", 1)
    p0_t = partner(p0, "leaf", 1)

    send2b, mine2 = call(
        sum2a_kernel, [((128, 256), BF), ((128, 256), F32)], (idx, keep2, recv2), 128 * 512, name="sum2a"
    )
    recv2b = partner(send2b, "leaf", 2)
    (pair1,) = call(sum1_kernel, [((128, 512), BF)], (keep1, recv1), 128 * 512, name="sum1")
    pair1_t = partner(pair1, "leaf", 2)
    (quad2,) = call(sum1_kernel, [((128, 256), BF)], (mine2, recv2b), 128 * 256, name="sum2b")
    quad2_t = partner(quad2, "leaf", 4)
    (a0,) = call(
        functools.partial(answer_kernel, 0),
        [((128, 1024), BF)],
        (idx, table, p0, p0_t),
        2 * 128 * 256 * 1024,
        name="answer0",
    )
    (a1h,) = call(
        functools.partial(answer_kernel, 1),
        [((128, 512), BF)],
        (idx, table, pair1, pair1_t),
        2 * 128 * 256 * 512,
        name="answer1",
    )
    a1o = partner(a1h, "leaf", 1)
    (a2q,) = call(
        functools.partial(answer_kernel, 2),
        [((128, 256), BF)],
        (idx, table, quad2, quad2_t),
        2 * 128 * 256 * 256,
        name="answer2",
    )
    a2q_t = partner(a2q, "leaf", 2)
    (a2h,) = call(join_kernel, [((128, 512), BF)], (idx, a2q, a2q_t), 128 * 512, name="join2")
    a2o = partner(a2h, "leaf", 1)
    (out,) = call(
        final_kernel,
        [((1024, 1024), BF)],
        (idx, *starts, correct, a0, a1h, a1o, a2h, a2o),
        2 * 1024 * 384 * 1024,
        limit=16 << 20,
        name="final",
    )
    return out


def solution(mesh):
    in_specs = (
        P("leaf", "rhs"),
        P(("leaf", "rhs"), None),
        P(None, "leaf", None),
        P(None, "leaf", None),
        P(None, "rhs", None),
        P(None, "rhs", None),
        P(None, "rhs", None),
    )
    out_specs = P("leaf", "rhs")
    return jax.shard_map(local, mesh=mesh, in_specs=in_specs, out_specs=out_specs, check_vma=False)
```

```python
import jax
import jax.numpy as jnp
from jax import lax
from jax.experimental import pallas as pl
from jax.experimental.pallas import tpu as pltpu
from jax.sharding import PartitionSpec as P

BF = jnp.bfloat16
F32 = jnp.float32
VMEM = pl.BlockSpec(memory_space=pltpu.VMEM)
ANY = pl.BlockSpec(memory_space=pl.ANY)
HBM = pl.BlockSpec(memory_space=pltpu.HBM)
MIB = 1 << 20


def partner(value, axis, mask):
    pairs = [(source, source ^ mask) for source in range(lax.axis_size(axis))]
    return lax.ppermute(value, axis, pairs)


def after(value, *others):
    return lax.optimization_barrier((value, *others))[0]


def mm(a, b):
    return lax.dot_general(a, b, (((1,), (0,)), ((), ())), preferred_element_type=F32)


def mm_nt(a, b):
    return lax.dot_general(a, b, (((1,), (1,)), ((), ())), preferred_element_type=F32)


def mm_tn(a, b):
    return lax.dot_general(a, b, (((0,), (0,)), ((), ())), preferred_element_type=F32)


def block(at, size):
    return pl.ds(pl.multiple_of(at * size, size), size)


def leaf_bits():
    leaf = lax.axis_index("leaf")
    return leaf & 1, leaf >> 1 & 1, leaf >> 2 & 1


def own_half():
    b0, _, b2 = leaf_bits()
    return b0 ^ b2


def call(body, outs, args, flops, name, specs=None, out_specs=None, scratch=(), limit=4, aliases=None):
    outs = [jax.ShapeDtypeStruct(s, d) for s, d in outs]
    size = sum(a.size * a.dtype.itemsize for a in args) + sum(
        o.size * o.dtype.itemsize for o in outs
    )
    return pl.pallas_call(
        body,
        out_shape=outs,
        in_specs=specs or [VMEM] * len(args),
        out_specs=out_specs or [VMEM] * len(outs),
        scratch_shapes=list(scratch),
        input_output_aliases=aliases or {},
        cost_estimate=pl.CostEstimate(flops=1024, bytes_accessed=1024, transcendentals=0),
        compiler_params=pltpu.CompilerParams(vmem_limit_bytes=limit * MIB),
        name=name,
    )(*args)


def pick_kernel(first, second, third, out_ref, sem):
    leaf = lax.axis_index("leaf")
    copies = [
        pltpu.make_async_copy(table.at[leaf >> level + 1], out_ref.at[level], sem.at[level])
        for level, table in enumerate((first, second, third))
    ]
    for copy in copies:
        copy.start()
    for copy in copies:
        copy.wait()


def cross_kernel(p_ref, c_ref, m_ref):
    m_ref[0] = mm_tn(p_ref[1], c_ref[0]).astype(BF)
    m_ref[1] = mm_tn(p_ref[2], c_ref[0]).astype(BF)
    m_ref[2] = mm_tn(p_ref[2], c_ref[1]).astype(BF)


def flip_kernel(p_ref, out_ref):
    rows = lax.broadcasted_iota(jnp.int32, (128, 128), 0)
    eye = (rows == lax.broadcasted_iota(jnp.int32, (128, 128), 1)).astype(BF)
    for level in range(3):
        out_ref[level * 128 : (level + 1) * 128] = mm_nt(eye, p_ref[level]).astype(BF)


def mix_kernel(k0, k1, k2, k3, m_ref, mt_ref, n_ref, nt_ref, rows_ref, mix_ref, full):
    r = lax.axis_index("rhs")
    bits = leaf_bits()
    for k, ref in enumerate((k0, k1, k2, k3)):
        for level in range(3):
            full[level, block(r ^ k, 64), :] = ref[level]
    for level, bit in enumerate(bits):
        rows_ref[level, :, 0:128] = full[level, block(bit, 128), block(bit, 128)]
        rows_ref[level, :, 128:256] = full[level, block(bit, 128), block(1 - bit, 128)]
    mine = rows_ref[0, :, 0:128]
    other = full[0, block(1 - bits[0], 128), block(bits[0], 128)]
    g = (mm(m_ref[0], mine) + mm(mt_ref[0], other)).astype(BF)
    h = mm(m_ref[1], mine) + mm(mt_ref[1], other)
    other = full[1, block(1 - bits[1], 128), block(bits[1], 128)]
    low = (mm(n_ref[...], rows_ref[1, :, 0:128]) + mm(nt_ref[...], other)).astype(BF)
    mix_ref[0] = g
    mix_ref[1] = low
    mix_ref[2] = (mm(low, g) - h).astype(BF)


def start_kernel(inv_ref, right_ref, s_ref):
    s_ref[...] = mm(inv_ref[...], right_ref[...]).astype(BF)


def part_kernel(f_ref, s0, s1, total_ref):
    r = lax.axis_index("rhs")
    total_ref[...] = mm(f_ref[:, block(r, 256)], s0[...]) + mm(f_ref[:, block(r ^ 1, 256)], s1[...])


def late_kernel(inv_ref, right_ref, f_ref, total_ref, s_ref, out_ref):
    rows = block(lax.axis_index("rhs") ^ 2, 256)
    s_ref[...] = mm(inv_ref[...], right_ref[...]).astype(BF)
    out_ref[...] = total_ref[...] + mm(f_ref[:, rows], s_ref[...])


def project_kernel(
    inv_ref, right_ref, f_ref, total_ref, mix_ref, s_ref, p0_ref, send2, send1, keep2, keep1
):
    rows = block(lax.axis_index("rhs") ^ 3, 256)
    half = own_half()
    for part in range(2):
        cols = block(half ^ (1 - part), 512)
        start = mm(inv_ref[...], right_ref[:, cols]).astype(BF)
        s_ref[:, cols] = start
        total = total_ref[:, cols] + mm(f_ref[:, rows], start)
        raw0, raw1 = total[0:128].astype(BF), total[128:256].astype(BF)
        p0_ref[:, cols] = raw0
        one = total[128:256] - mm(mix_ref[0], raw0)
        two = total[256:384] - mm(mix_ref[1], raw1) + mm(mix_ref[2], raw0)
        if part == 0:
            send1[...] = one.astype(BF)
            send2[...] = two.astype(BF)
        else:
            keep1[...] = one
            keep2[...] = two


def answer_kernel(level):
    def body(k_ref, mine_ref, other_ref, out_ref):
        own, other = k_ref[level, :, 0:128], k_ref[level, :, 128:256]
        out_ref[...] = (mm(own, mine_ref[...]) + mm(other, other_ref[...])).astype(BF)

    return body


def near_kernel(s0, s1, s2, s3, c_ref, a0, a1h, a2h, out_ref, rest_ref, done, sem):
    r = lax.axis_index("rhs")
    half = own_half()
    cols, far = block(half, 512), block(1 - half, 512)
    copies = []
    for k, ref in enumerate((s0, s1, s2, s3)):
        rows = block(r ^ k, 256)
        value = ref[:, cols].astype(F32) - mm(c_ref[0, rows], a0[:, cols])
        value = value - mm(c_ref[1, rows], a1h[...]) - mm(c_ref[2, rows], a2h[...])
        done[k] = value.astype(BF)
        copy = pltpu.make_async_copy(done.at[k], out_ref.at[rows, cols], sem.at[k])
        copy.start()
        copies.append(copy)
    for k, ref in enumerate((s0, s1, s2, s3)):
        rows = block(r ^ k, 256)
        rest_ref[rows] = ref[:, far].astype(F32) - mm(c_ref[0, rows], a0[:, far])
    for copy in copies:
        copy.wait()


def far_kernel(rest_ref, c_ref, a1o, a2o, near_ref, out_ref, done, sem):
    far = block(1 - own_half(), 512)
    copies = []
    for k in range(4):
        rows = pl.ds(k * 256, 256)
        value = rest_ref[rows] - mm(c_ref[1, rows], a1o[...]) - mm(c_ref[2, rows], a2o[...])
        done[k] = value.astype(BF)
        copy = pltpu.make_async_copy(done.at[k], out_ref.at[rows, far], sem.at[k])
        copy.start()
        copies.append(copy)
    for copy in copies:
        copy.wait()


def local(right, inverse, project, correct, first, second, third):
    inv_y = partner(inverse, "rhs", 2)
    (cross,) = call(
        cross_kernel, [((3, 128, 128), BF)], (project, correct), 6 * 128 * 128 * 1024, "cross"
    )
    cross_t = partner(cross, "leaf", 1)
    (nodes,) = call(
        pick_kernel,
        [((3, 64, 256), BF)],
        (first, second, third),
        0,
        "pick",
        specs=[HBM] * 3,
        limit=58,
        scratch=[pltpu.SemaphoreType.DMA((3,))],
    )
    nodes_y = partner(nodes, "rhs", 2)
    nodes_c = partner(nodes, "rhs", 1)
    inv_c = partner(inverse, "rhs", 1)
    low = (cross[2].astype(F32) + cross_t[2].astype(F32)).astype(BF)
    low_t = partner(low, "leaf", 2)

    square = 2 * 256 * 1024 * 1024
    (factors,) = call(flip_kernel, [((384, 1024), BF)], (project,), square // 4, "flip")
    (s0,) = call(start_kernel, [((256, 1024), BF)], (inverse, right), square, "start0", limit=6)
    (s1,) = call(start_kernel, [((256, 1024), BF)], (inv_c, right), square, "start1", limit=6)
    (total,) = call(
        part_kernel, [((384, 1024), F32)], (factors, s0, s1), square, "part", limit=8
    )
    inv_y, nodes_y = lax.optimization_barrier((inv_y, nodes_y, total, low_t))[:2]
    nodes_yc = partner(nodes_y, "rhs", 1)
    inv_yc = partner(inv_y, "rhs", 1)
    s2, total = call(
        late_kernel,
        [((256, 1024), BF), ((384, 1024), F32)],
        (inv_y, right, factors, total),
        square,
        "late",
        limit=10,
    )
    nodes_yc = after(nodes_yc, inv_yc)
    rows, mix = call(
        mix_kernel,
        [((3, 128, 256), BF), ((3, 128, 128), BF)],
        (nodes, nodes_c, nodes_y, nodes_yc, cross, cross_t, low, low_t),
        8 * 128**3,
        "mix",
        scratch=[pltpu.VMEM((3, 256, 256), BF)],
    )
    s3, p0, send2, send1, keep2, keep1 = call(
        project_kernel,
        [
            ((256, 1024), BF),
            ((128, 1024), BF),
            ((128, 512), BF),
            ((128, 512), BF),
            ((128, 512), F32),
            ((128, 512), F32),
        ],
        (inv_yc, right, factors, total, mix),
        square,
        "project",
        limit=10,
    )

    recv2 = partner(send2, "leaf", 1)
    recv1 = partner(send1, "leaf", 1)
    pair2 = keep2 + recv2.astype(F32)
    pair2_b = pair2.astype(BF)
    pair2_t = partner(pair2_b, "leaf", 2)
    pair1 = (keep1 + after(recv1, pair2_b).astype(F32)).astype(BF)
    pair1_t = partner(pair1, "leaf", 2)
    quad2 = (pair2 + pair2_t.astype(F32)).astype(BF)
    quad2_t = partner(quad2, "leaf", 7)
    p0 = after(p0, quad2)
    p0_t = partner(p0, "leaf", 1)

    pair1_t = after(pair1_t, quad2)
    (a1h,) = call(
        answer_kernel(1), [((128, 512), BF)], (rows, pair1, pair1_t), 2**17 * 256, "answer1"
    )
    a1o = partner(a1h, "leaf", 1)
    (a2h,) = call(
        answer_kernel(2), [((128, 512), BF)], (rows, quad2, quad2_t), 2**17 * 256, "answer2"
    )
    a2o = partner(a2h, "leaf", 1)
    p0_t = after(p0_t, a2h)
    (a0,) = call(answer_kernel(0), [((128, 1024), BF)], (rows, p0, p0_t), 2**18 * 256, "answer0")

    near, rest = call(
        near_kernel,
        [((1024, 1024), BF), ((1024, 512), F32)],
        (s0, s1, s2, s3, correct, a0, a1h, a2h),
        2 * 1024 * 256 * 1024,
        "near",
        out_specs=[ANY, VMEM],
        scratch=[pltpu.VMEM((4, 256, 512), BF), pltpu.SemaphoreType.DMA((4,))],
        limit=12,
    )
    (out,) = call(
        far_kernel,
        [((1024, 1024), BF)],
        (rest, correct, a1o, a2o, near),
        2 * 1024 * 128 * 1024,
        "far",
        specs=[VMEM, VMEM, VMEM, VMEM, ANY],
        out_specs=[ANY],
        scratch=[pltpu.VMEM((4, 256, 512), BF), pltpu.SemaphoreType.DMA((4,))],
        limit=8,
        aliases={4: 0},
    )
    return out


def solution(mesh):
    in_specs = (
        P("leaf", "rhs"),
        P(("leaf", "rhs"), None),
        P(None, "leaf", None),
        P(None, "leaf", None),
        P(None, "rhs", None),
        P(None, "rhs", None),
        P(None, "rhs", None),
    )
    out_specs = P("leaf", "rhs")
    return jax.shard_map(local, mesh=mesh, in_specs=in_specs, out_specs=out_specs, check_vma=False)
```

```python
import jax
import jax.numpy as jnp
from jax import lax
from jax.experimental import pallas as pl
from jax.experimental.pallas import tpu as pltpu
from jax.sharding import PartitionSpec as P

BF = jnp.bfloat16
F32 = jnp.float32
VMEM = pl.BlockSpec(memory_space=pltpu.VMEM)
ANY = pl.BlockSpec(memory_space=pl.ANY)
HBM = pl.BlockSpec(memory_space=pltpu.HBM)
MIB = 1 << 20


def partner(value, axis, mask):
    pairs = [(source, source ^ mask) for source in range(lax.axis_size(axis))]
    return lax.ppermute(value, axis, pairs)


def after(value, *others):
    return lax.optimization_barrier((value, *others))[0]


def mm(a, b):
    return lax.dot_general(a, b, (((1,), (0,)), ((), ())), preferred_element_type=F32)


def mm_nt(a, b):
    return lax.dot_general(a, b, (((1,), (1,)), ((), ())), preferred_element_type=F32)


def mm_tn(a, b):
    return lax.dot_general(a, b, (((0,), (0,)), ((), ())), preferred_element_type=F32)


def block(at, size):
    return pl.ds(pl.multiple_of(at * size, size), size)


def leaf_bits():
    leaf = lax.axis_index("leaf")
    return leaf & 1, leaf >> 1 & 1, leaf >> 2 & 1


def own_half():
    b0, _, b2 = leaf_bits()
    return b0 ^ b2


def call(body, outs, args, flops, name, specs=None, out_specs=None, scratch=(), limit=4, aliases=None):
    outs = [jax.ShapeDtypeStruct(s, d) for s, d in outs]
    size = sum(a.size * a.dtype.itemsize for a in args) + sum(
        o.size * o.dtype.itemsize for o in outs
    )
    return pl.pallas_call(
        body,
        out_shape=outs,
        in_specs=specs or [VMEM] * len(args),
        out_specs=out_specs or [VMEM] * len(outs),
        scratch_shapes=list(scratch),
        input_output_aliases=aliases or {},
        cost_estimate=pl.CostEstimate(flops=1024, bytes_accessed=1024, transcendentals=0),
        compiler_params=pltpu.CompilerParams(vmem_limit_bytes=limit * MIB),
        name=name,
    )(*args)


def pick_kernel(first, second, third, out_ref, sem):
    leaf = lax.axis_index("leaf")
    copies = [
        pltpu.make_async_copy(table.at[leaf >> level + 1], out_ref.at[level], sem.at[level])
        for level, table in enumerate((first, second, third))
    ]
    for copy in copies:
        copy.start()
    for copy in copies:
        copy.wait()


def cross_kernel(p_ref, c_ref, m_ref):
    m_ref[0] = mm_tn(p_ref[1], c_ref[0]).astype(BF)
    m_ref[1] = mm_tn(p_ref[2], c_ref[0]).astype(BF)
    m_ref[2] = mm_tn(p_ref[2], c_ref[1]).astype(BF)


def flip_kernel(p_ref, out_ref):
    rows = lax.broadcasted_iota(jnp.int32, (128, 128), 0)
    eye = (rows == lax.broadcasted_iota(jnp.int32, (128, 128), 1)).astype(BF)
    for level in range(3):
        out_ref[level * 128 : (level + 1) * 128] = mm_nt(eye, p_ref[level]).astype(BF)


def mix_kernel(k0, k1, k2, k3, m_ref, mt_ref, n_ref, nt_ref, rows_ref, mix_ref, full):
    r = lax.axis_index("rhs")
    bits = leaf_bits()
    for k, ref in enumerate((k0, k1, k2, k3)):
        for level in range(3):
            full[level, block(r ^ k, 64), :] = ref[level]
    for level, bit in enumerate(bits):
        rows_ref[level, :, 0:128] = full[level, block(bit, 128), block(bit, 128)]
        rows_ref[level, :, 128:256] = full[level, block(bit, 128), block(1 - bit, 128)]
    mine = rows_ref[0, :, 0:128]
    other = full[0, block(1 - bits[0], 128), block(bits[0], 128)]
    g = (mm(m_ref[0], mine) + mm(mt_ref[0], other)).astype(BF)
    h = mm(m_ref[1], mine) + mm(mt_ref[1], other)
    other = full[1, block(1 - bits[1], 128), block(bits[1], 128)]
    low = (mm(n_ref[...], rows_ref[1, :, 0:128]) + mm(nt_ref[...], other)).astype(BF)
    mix_ref[0] = g
    mix_ref[1] = low
    mix_ref[2] = (mm(low, g) - h).astype(BF)


def start_kernel(inv_ref, right_ref, s_ref):
    s_ref[...] = mm(inv_ref[...], right_ref[...]).astype(BF)


def part_kernel(f_ref, s0, s1, total_ref):
    r = lax.axis_index("rhs")
    total_ref[...] = mm(f_ref[:, block(r, 256)], s0[...]) + mm(f_ref[:, block(r ^ 1, 256)], s1[...])


def late_kernel(inv_ref, right_ref, f_ref, total_ref, s_ref, out_ref):
    rows = block(lax.axis_index("rhs") ^ 2, 256)
    s_ref[...] = mm(inv_ref[...], right_ref[...]).astype(BF)
    out_ref[...] = total_ref[...] + mm(f_ref[:, rows], s_ref[...])


def project_kernel(
    inv_ref, right_ref, f_ref, total_ref, mix_ref, s_ref, p0_ref, send2, send1, keep2, keep1
):
    rows = block(lax.axis_index("rhs") ^ 3, 256)
    half = own_half()
    for part in range(2):
        cols = block(half ^ (1 - part), 512)
        start = mm(inv_ref[...], right_ref[:, cols]).astype(BF)
        s_ref[:, cols] = start
        total = total_ref[:, cols] + mm(f_ref[:, rows], start)
        raw0, raw1 = total[0:128].astype(BF), total[128:256].astype(BF)
        p0_ref[:, cols] = raw0
        one = total[128:256] - mm(mix_ref[0], raw0)
        two = total[256:384] - mm(mix_ref[1], raw1) + mm(mix_ref[2], raw0)
        if part == 0:
            send1[...] = one.astype(BF)
            send2[...] = two.astype(BF)
        else:
            keep1[...] = one
            keep2[...] = two


def answer_kernel(level):
    def body(k_ref, mine_ref, other_ref, out_ref):
        own, other = k_ref[level, :, 0:128], k_ref[level, :, 128:256]
        out_ref[...] = (mm(own, mine_ref[...]) + mm(other, other_ref[...])).astype(BF)

    return body


def near_kernel(s0, s1, s2, s3, c_ref, a0, a1h, a1o, a2h, out_ref, rest_ref, done, sem):
    r = lax.axis_index("rhs")
    half = own_half()
    cols, far = block(half, 512), block(1 - half, 512)
    copies = []
    for k, ref in enumerate((s0, s1, s2, s3)):
        rows = block(r ^ k, 256)
        value = ref[:, cols].astype(F32) - mm(c_ref[0, rows], a0[:, cols])
        value = value - mm(c_ref[1, rows], a1h[...]) - mm(c_ref[2, rows], a2h[...])
        done[k] = value.astype(BF)
        copy = pltpu.make_async_copy(done.at[k], out_ref.at[rows, cols], sem.at[k])
        copy.start()
        copies.append(copy)
    for k, ref in enumerate((s0, s1, s2, s3)):
        rows = block(r ^ k, 256)
        value = ref[:, far].astype(F32) - mm(c_ref[0, rows], a0[:, far])
        rest_ref[rows] = value - mm(c_ref[1, rows], a1o[...])
    for copy in copies:
        copy.wait()


def far_kernel(rest_ref, c_ref, a2o, near_ref, out_ref, done, sem):
    far = block(1 - own_half(), 512)
    copies = []
    for k in range(4):
        rows = pl.ds(k * 256, 256)
        done[k] = (rest_ref[rows] - mm(c_ref[2, rows], a2o[...])).astype(BF)
        copy = pltpu.make_async_copy(done.at[k], out_ref.at[rows, far], sem.at[k])
        copy.start()
        copies.append(copy)
    for copy in copies:
        copy.wait()


def local(right, inverse, project, correct, first, second, third):
    inv_y = partner(inverse, "rhs", 2)
    (cross,) = call(
        cross_kernel, [((3, 128, 128), BF)], (project, correct), 6 * 128 * 128 * 1024, "cross"
    )
    cross_t = partner(cross, "leaf", 1)
    (nodes,) = call(
        pick_kernel,
        [((3, 64, 256), BF)],
        (first, second, third),
        0,
        "pick",
        specs=[HBM] * 3,
        limit=58,
        scratch=[pltpu.SemaphoreType.DMA((3,))],
    )
    nodes_y = partner(nodes, "rhs", 2)
    nodes_c = partner(nodes, "rhs", 1)
    inv_c = partner(inverse, "rhs", 1)
    low = (cross[2].astype(F32) + cross_t[2].astype(F32)).astype(BF)
    low_t = partner(low, "leaf", 2)

    square = 2 * 256 * 1024 * 1024
    (factors,) = call(flip_kernel, [((384, 1024), BF)], (project,), square // 4, "flip")
    (s0,) = call(start_kernel, [((256, 1024), BF)], (inverse, right), square, "start0", limit=6)
    (s1,) = call(start_kernel, [((256, 1024), BF)], (inv_c, right), square, "start1", limit=6)
    (total,) = call(
        part_kernel, [((384, 1024), F32)], (factors, s0, s1), square, "part", limit=8
    )
    inv_y, nodes_y = lax.optimization_barrier((inv_y, nodes_y, total, low_t))[:2]
    nodes_yc = partner(nodes_y, "rhs", 1)
    inv_yc = partner(inv_y, "rhs", 1)
    s2, total = call(
        late_kernel,
        [((256, 1024), BF), ((384, 1024), F32)],
        (inv_y, right, factors, total),
        square,
        "late",
        limit=10,
    )
    nodes_yc = after(nodes_yc, inv_yc)
    rows, mix = call(
        mix_kernel,
        [((3, 128, 256), BF), ((3, 128, 128), BF)],
        (nodes, nodes_c, nodes_y, nodes_yc, cross, cross_t, low, low_t),
        8 * 128**3,
        "mix",
        scratch=[pltpu.VMEM((3, 256, 256), BF)],
    )
    s3, p0, send2, send1, keep2, keep1 = call(
        project_kernel,
        [
            ((256, 1024), BF),
            ((128, 1024), BF),
            ((128, 512), BF),
            ((128, 512), BF),
            ((128, 512), F32),
            ((128, 512), F32),
        ],
        (inv_yc, right, factors, total, mix),
        square,
        "project",
        limit=10,
    )

    recv2 = partner(send2, "leaf", 1)
    recv1 = partner(send1, "leaf", 1)
    pair2 = keep2 + recv2.astype(F32)
    pair2_b = pair2.astype(BF)
    pair2_t = partner(pair2_b, "leaf", 2)
    pair1 = (keep1 + after(recv1, pair2_b).astype(F32)).astype(BF)
    pair1_t = partner(pair1, "leaf", 2)
    quad2 = (pair2 + pair2_t.astype(F32)).astype(BF)
    quad2_t = partner(quad2, "leaf", 7)
    p0 = after(p0, pair2_b)
    p0_t = partner(p0, "leaf", 1)

    pair1_t = after(pair1_t, quad2)
    (a1h,) = call(
        answer_kernel(1), [((128, 512), BF)], (rows, pair1, pair1_t), 2**17 * 256, "answer1"
    )
    a1o = partner(a1h, "leaf", 1)
    (a0,) = call(answer_kernel(0), [((128, 1024), BF)], (rows, p0, p0_t), 2**18 * 256, "answer0")
    quad2_t = after(quad2_t, a0)
    (a2h,) = call(
        answer_kernel(2), [((128, 512), BF)], (rows, quad2, quad2_t), 2**17 * 256, "answer2"
    )
    a2o = partner(a2h, "leaf", 1)

    near, rest = call(
        near_kernel,
        [((1024, 1024), BF), ((1024, 512), F32)],
        (s0, s1, s2, s3, correct, a0, a1h, a1o, a2h),
        2 * 1024 * 256 * 1024,
        "near",
        out_specs=[ANY, VMEM],
        scratch=[pltpu.VMEM((4, 256, 512), BF), pltpu.SemaphoreType.DMA((4,))],
        limit=12,
    )
    (out,) = call(
        far_kernel,
        [((1024, 1024), BF)],
        (rest, correct, a2o, near),
        2 * 1024 * 128 * 1024,
        "far",
        specs=[VMEM, VMEM, VMEM, ANY],
        out_specs=[ANY],
        scratch=[pltpu.VMEM((4, 256, 512), BF), pltpu.SemaphoreType.DMA((4,))],
        limit=8,
        aliases={3: 0},
    )
    return out


def solution(mesh):
    in_specs = (
        P("leaf", "rhs"),
        P(("leaf", "rhs"), None),
        P(None, "leaf", None),
        P(None, "leaf", None),
        P(None, "rhs", None),
        P(None, "rhs", None),
        P(None, "rhs", None),
    )
    out_specs = P("leaf", "rhs")
    return jax.shard_map(local, mesh=mesh, in_specs=in_specs, out_specs=out_specs, check_vma=False)
```

```python
import jax
import jax.numpy as jnp
from jax import lax
from jax.experimental import pallas as pl
from jax.experimental.pallas import tpu as pltpu
from jax.sharding import PartitionSpec as P

BF = jnp.bfloat16
F32 = jnp.float32
VMEM = pl.BlockSpec(memory_space=pltpu.VMEM)
ANY = pl.BlockSpec(memory_space=pl.ANY)
HBM = pl.BlockSpec(memory_space=pltpu.HBM)
MIB = 1 << 20


def partner(value, axis, mask):
    pairs = [(source, source ^ mask) for source in range(lax.axis_size(axis))]
    return lax.ppermute(value, axis, pairs)


def after(value, *others):
    return lax.optimization_barrier((value, *others))[0]


def mm(a, b):
    return lax.dot_general(a, b, (((1,), (0,)), ((), ())), preferred_element_type=F32)


def mm_nt(a, b):
    return lax.dot_general(a, b, (((1,), (1,)), ((), ())), preferred_element_type=F32)


def mm_tn(a, b):
    return lax.dot_general(a, b, (((0,), (0,)), ((), ())), preferred_element_type=F32)


def block(at, size):
    return pl.ds(pl.multiple_of(at * size, size), size)


def leaf_bits():
    leaf = lax.axis_index("leaf")
    return leaf & 1, leaf >> 1 & 1, leaf >> 2 & 1


def own_half():
    return leaf_bits()[0]


def call(body, outs, args, flops, name, specs=None, out_specs=None, scratch=(), limit=4, aliases=None):
    outs = [jax.ShapeDtypeStruct(s, d) for s, d in outs]
    size = sum(a.size * a.dtype.itemsize for a in args) + sum(
        o.size * o.dtype.itemsize for o in outs
    )
    return pl.pallas_call(
        body,
        out_shape=outs,
        in_specs=specs or [VMEM] * len(args),
        out_specs=out_specs or [VMEM] * len(outs),
        scratch_shapes=list(scratch),
        input_output_aliases=aliases or {},
        cost_estimate=pl.CostEstimate(flops=1024, bytes_accessed=1024, transcendentals=0),
        compiler_params=pltpu.CompilerParams(vmem_limit_bytes=limit * MIB),
        name=name,
    )(*args)


def pick_kernel(first, second, third, out_ref, cols_ref, sem):
    leaf = lax.axis_index("leaf")
    bits = leaf_bits()
    copies = [
        pltpu.make_async_copy(table.at[leaf >> level + 1], out_ref.at[level], sem.at[level])
        for level, table in enumerate((first, second, third))
    ]
    for level, table in enumerate((first, second)):
        source = table.at[leaf >> level + 1, :, block(bits[level], 128)]
        copies.append(pltpu.make_async_copy(source, cols_ref.at[level], sem.at[3 + level]))
    for copy in copies:
        copy.start()
    for copy in copies:
        copy.wait()


def cross_kernel(p_ref, c_ref, m_ref):
    m_ref[0] = mm_tn(p_ref[1], c_ref[0]).astype(BF)
    m_ref[1] = mm_tn(p_ref[2], c_ref[0]).astype(BF)
    m_ref[2] = mm_tn(p_ref[2], c_ref[1]).astype(BF)


def flip_kernel(p_ref, out_ref):
    rows = lax.broadcasted_iota(jnp.int32, (128, 128), 0)
    eye = (rows == lax.broadcasted_iota(jnp.int32, (128, 128), 1)).astype(BF)
    for level in range(3):
        out_ref[level * 128 : (level + 1) * 128] = mm_nt(eye, p_ref[level]).astype(BF)


def mix_kernel(k0, k1, k2, k3, m_ref, mt_ref, n_ref, nt_ref, mix_ref, full):
    r = lax.axis_index("rhs")
    b0, b1, _ = leaf_bits()
    for k, ref in enumerate((k0, k1, k2, k3)):
        for level in range(2):
            full[level, block(r ^ k, 64), :] = ref[level]
    mine, other = full[0, block(b0, 128), :], full[0, block(1 - b0, 128), :]
    g = (mm(m_ref[0], mine) + mm(mt_ref[0], other)).astype(BF)
    h = mm(m_ref[1], mine) + mm(mt_ref[1], other)
    mine, other = full[1, block(b1, 128), :], full[1, block(1 - b1, 128), :]
    low = (mm(n_ref[...], mine) + mm(nt_ref[...], other)).astype(BF)
    mix_ref[0] = g
    mix_ref[1] = low
    mix_ref[2] = (mm(low, g) - h).astype(BF)


def rows_kernel(k0, k1, k2, k3, rows_ref, full):
    r = lax.axis_index("rhs")
    for k, ref in enumerate((k0, k1, k2, k3)):
        for level in range(3):
            full[level, block(r ^ k, 64), :] = ref[level]
    for level, bit in enumerate(leaf_bits()):
        rows_ref[level, :, 0:128] = full[level, block(bit, 128), block(bit, 128)]
        rows_ref[level, :, 128:256] = full[level, block(bit, 128), block(1 - bit, 128)]


def start_kernel(inv_ref, right_ref, s_ref):
    s_ref[...] = mm(inv_ref[...], right_ref[...]).astype(BF)


def part_kernel(f_ref, s0, s1, total_ref):
    r = lax.axis_index("rhs")
    total_ref[...] = mm(f_ref[:, block(r, 256)], s0[...]) + mm(f_ref[:, block(r ^ 1, 256)], s1[...])


def late_kernel(inv_ref, right_ref, f_ref, total_ref, s_ref, out_ref):
    rows = block(lax.axis_index("rhs") ^ 2, 256)
    s_ref[...] = mm(inv_ref[...], right_ref[...]).astype(BF)
    out_ref[...] = total_ref[...] + mm(f_ref[:, rows], s_ref[...])


def project_part(half, inv_ref, right_ref, f_ref, total_ref, mix_ref, s_ref):
    rows = block(lax.axis_index("rhs") ^ 3, 256)
    cols = block(half, 512)
    start = mm(inv_ref[...], right_ref[:, cols]).astype(BF)
    s_ref[...] = start
    total = total_ref[:, cols] + mm(f_ref[:, rows], start)
    raw0, raw1 = total[0:128].astype(BF), total[128:256].astype(BF)
    one = total[128:256] - mm(mix_ref[0], raw0)
    two = total[256:384] - mm(mix_ref[1], raw1) + mm(mix_ref[2], raw0)
    return raw0, one, two


def send_kernel(inv_ref, right_ref, f_ref, total_ref, mix_ref, s_ref, far0, send2, send1):
    half = 1 - own_half()
    raw0, one, two = project_part(half, inv_ref, right_ref, f_ref, total_ref, mix_ref, s_ref)
    far0[...] = raw0
    send1[...] = one.astype(BF)
    send2[...] = two.astype(BF)


def keep_kernel(inv_ref, right_ref, f_ref, total_ref, mix_ref, far0, s_ref, p0_ref, keep2, keep1):
    half = own_half()
    raw0, one, two = project_part(half, inv_ref, right_ref, f_ref, total_ref, mix_ref, s_ref)
    p0_ref[:, block(half, 512)] = raw0
    p0_ref[:, block(1 - half, 512)] = far0[...]
    keep1[...] = one
    keep2[...] = two


def answer_kernel(level):
    def body(k_ref, mine_ref, other_ref, out_ref):
        own, other = k_ref[level, :, 0:128], k_ref[level, :, 128:256]
        out_ref[...] = (mm(own, mine_ref[...]) + mm(other, other_ref[...])).astype(BF)

    return body


def near_kernel(s0, s1, s2, s3n, s3f, c_ref, a0, a1h, a1o, a2h, out_ref, rest_ref, done, sem):
    r = lax.axis_index("rhs")
    half = own_half()
    cols, far = block(half, 512), block(1 - half, 512)
    copies = []
    for k, ref in enumerate((s0, s1, s2, s3n)):
        rows = block(r ^ k, 256)
        start = ref[...] if k == 3 else ref[:, cols]
        value = start.astype(F32) - mm(c_ref[0, rows], a0[:, cols])
        value = value - mm(c_ref[1, rows], a1h[...]) - mm(c_ref[2, rows], a2h[...])
        done[k] = value.astype(BF)
        copy = pltpu.make_async_copy(done.at[k], out_ref.at[rows, cols], sem.at[k])
        copy.start()
        copies.append(copy)
    for k, ref in enumerate((s0, s1, s2, s3f)):
        rows = block(r ^ k, 256)
        start = ref[...] if k == 3 else ref[:, far]
        value = start.astype(F32) - mm(c_ref[0, rows], a0[:, far])
        rest_ref[rows] = value - mm(c_ref[1, rows], a1o[...])
    for copy in copies:
        copy.wait()


def far_kernel(rest_ref, c_ref, a2o, near_ref, out_ref, done, sem):
    far = block(1 - own_half(), 512)
    copies = []
    for k in range(4):
        rows = pl.ds(k * 256, 256)
        done[k] = (rest_ref[rows] - mm(c_ref[2, rows], a2o[...])).astype(BF)
        copy = pltpu.make_async_copy(done.at[k], out_ref.at[rows, far], sem.at[k])
        copy.start()
        copies.append(copy)
    for copy in copies:
        copy.wait()


def local(right, inverse, project, correct, first, second, third):
    inv_y = partner(inverse, "rhs", 2)
    (cross,) = call(
        cross_kernel, [((3, 128, 128), BF)], (project, correct), 6 * 128 * 128 * 1024, "cross"
    )
    cross_t = partner(cross, "leaf", 1)
    nodes, cols = call(
        pick_kernel,
        [((3, 64, 256), BF), ((2, 64, 128), BF)],
        (first, second, third),
        0,
        "pick",
        specs=[HBM] * 3,
        limit=58,
        scratch=[pltpu.SemaphoreType.DMA((5,))],
    )
    cols_y = partner(cols, "rhs", 2)
    cols_c = partner(cols, "rhs", 1)
    inv_c = partner(inverse, "rhs", 1)
    low = (cross[2].astype(F32) + cross_t[2].astype(F32)).astype(BF)
    low_t = partner(low, "leaf", 2)

    square = 2 * 256 * 1024 * 1024
    (factors,) = call(flip_kernel, [((384, 1024), BF)], (project,), square // 4, "flip")
    (s0,) = call(start_kernel, [((256, 1024), BF)], (inverse, right), square, "start0", limit=6)
    (s1,) = call(start_kernel, [((256, 1024), BF)], (inv_c, right), square, "start1", limit=6)
    (total,) = call(
        part_kernel, [((384, 1024), F32)], (factors, s0, s1), square, "part", limit=8
    )
    inv_y, cols_y = lax.optimization_barrier((inv_y, cols_y, total, low_t))[:2]
    cols_yc = partner(cols_y, "rhs", 1)
    inv_yc = partner(inv_y, "rhs", 1)
    s2, total = call(
        late_kernel,
        [((256, 1024), BF), ((384, 1024), F32)],
        (inv_y, right, factors, total),
        square,
        "late",
        limit=10,
    )
    cols_yc = after(cols_yc, inv_yc)
    (mix,) = call(
        mix_kernel,
        [((3, 128, 128), BF)],
        (cols, cols_c, cols_y, cols_yc, cross, cross_t, low, low_t),
        8 * 128**3,
        "mix",
        scratch=[pltpu.VMEM((2, 256, 128), BF)],
    )
    short, long = ((128, 512), BF), ((128, 512), F32)
    s3f, far0, send2, send1 = call(
        send_kernel,
        [((256, 512), BF), short, short, short],
        (inv_yc, right, factors, total, mix),
        square // 2,
        "send",
        limit=10,
    )
    s3n, p0, keep2, keep1 = call(
        keep_kernel,
        [((256, 512), BF), ((128, 1024), BF), long, long],
        (inv_yc, right, factors, total, mix, far0),
        square // 2,
        "keep",
        limit=10,
    )

    recv2 = partner(send2, "leaf", 1)
    recv1 = partner(send1, "leaf", 1)
    pair2 = keep2 + recv2.astype(F32)
    pair2_b = pair2.astype(BF)
    pair2_t = partner(pair2_b, "leaf", 2)
    nodes_y = partner(after(nodes, pair2_b), "rhs", 2)
    pair1 = (keep1 + after(recv1, pair2_b).astype(F32)).astype(BF)
    pair1_t = partner(pair1, "leaf", 2)
    quad2 = (pair2 + pair2_t.astype(F32)).astype(BF)
    quad2_t = partner(quad2, "leaf", 6)
    p0 = after(p0, pair2_b)
    p0_t = partner(p0, "leaf", 1)

    nodes_c = partner(after(nodes, quad2), "rhs", 1)
    nodes_yc = partner(after(nodes_y, quad2), "rhs", 1)
    (rows,) = call(
        rows_kernel,
        [((3, 128, 256), BF)],
        (nodes, nodes_c, nodes_y, nodes_yc),
        1024,
        "rows",
        scratch=[pltpu.VMEM((3, 256, 256), BF)],
    )
    pair1_t = after(pair1_t, quad2, rows)
    (a1h,) = call(
        answer_kernel(1), [((128, 512), BF)], (rows, pair1, pair1_t), 2**17 * 256, "answer1"
    )
    a1o = partner(a1h, "leaf", 1)
    (a0,) = call(answer_kernel(0), [((128, 1024), BF)], (rows, p0, p0_t), 2**18 * 256, "answer0")
    quad2_t = after(quad2_t, a0)
    (a2h,) = call(
        answer_kernel(2), [((128, 512), BF)], (rows, quad2, quad2_t), 2**17 * 256, "answer2"
    )
    a2o = partner(a2h, "leaf", 1)

    near, rest = call(
        near_kernel,
        [((1024, 1024), BF), ((1024, 512), F32)],
        (s0, s1, s2, s3n, s3f, correct, a0, a1h, a1o, a2h),
        2 * 1024 * 256 * 1024,
        "near",
        out_specs=[ANY, VMEM],
        scratch=[pltpu.VMEM((4, 256, 512), BF), pltpu.SemaphoreType.DMA((4,))],
        limit=12,
    )
    (out,) = call(
        far_kernel,
        [((1024, 1024), BF)],
        (rest, correct, a2o, near),
        2 * 1024 * 128 * 1024,
        "far",
        specs=[VMEM, VMEM, VMEM, ANY],
        out_specs=[ANY],
        scratch=[pltpu.VMEM((4, 256, 512), BF), pltpu.SemaphoreType.DMA((4,))],
        limit=8,
        aliases={3: 0},
    )
    return out


def solution(mesh):
    in_specs = (
        P("leaf", "rhs"),
        P(("leaf", "rhs"), None),
        P(None, "leaf", None),
        P(None, "leaf", None),
        P(None, "rhs", None),
        P(None, "rhs", None),
        P(None, "rhs", None),
    )
    out_specs = P("leaf", "rhs")
    return jax.shard_map(local, mesh=mesh, in_specs=in_specs, out_specs=out_specs, check_vma=False)
```
